32 devices in a mesh: dp: 4 (over y, x), expert: 4 (over z), tensor: 2 (over core).
Axes of the slice: x: 2, y: 2, z: 4, core: 2. Of those that a mesh axis runs over, the one named last changes fastest.
Arguments:
- tokens: bfloat16 [2048, 2048], P(('dp', 'expert'), 'tensor'), may hold values from -6 to 6
- norm_gain: bfloat16 [2048], replicated, may hold values from 0.25 to 1.75
- expert_ids: int32 [2048, 2], P(('dp', 'expert')), may hold values from 0 to 3, all different within a row; in each aligned block of 128 rows (0 to 127, 128 to 255, ...) at most 128 rows name the same one
- gate_codes: int32 [2048, 2], P(('dp', 'expert')), may hold values from 1 to 255
- gate_weights: bfloat16 [4, 7168, 2048], P('expert', ('dp', 'tensor')), may hold values from -0.125 to 0.125
- up_weights: bfloat16 [4, 7168, 2048], P('expert', ('dp', 'tensor')), may hold values from -0.125 to 0.125
- down_weights: bfloat16 [4, 7168, 2048], P('expert', ('dp', 'tensor')), may hold values from -0.0625 to 0.0625
- value_head: bfloat16 [2048, 128], replicated, may hold values from -0.125 to 0.125
- actions: int32 [2048], P(('dp', 'expert')), may hold values from 0 to 127
- rewards: int32 [2048], P(('dp', 'expert')), may hold values from -8 to 8
- trace_codes: int32 [2048], P(('dp', 'expert')), may hold values from 1 to 1024
Outputs:
- action_values: float32 [2048, 128], P(('dp', 'expert'))
- retrace_targets: float32 [2048], P(('dp', 'expert'))
The draws below stay inside these ranges and needn't reach their ends.
Inputs may be any that keep to these rules, and one draw needn't show every extreme that they name: `expert_ids`: each row names 2 different experts; within the 128 rows of one index pair of dp and expert each expert is named by at most 128 rows, and in some of these blocks one expert by exactly 128.
All inputs are finite; a program needn't handle non-finite values.
Results may differ from the reference program's by a relative error of at most 0.005.
Values may be sent and summed in bfloat16 or wider, within the bound.
No kernel may reach another device: no remote copies, remote signals or barrier semaphores. Data moves between devices by JAX's collectives and lax.ppermute only.
A program may use at most 256 MiB of HBM per device.

```python
import math
import jax
import jax.numpy as jnp
import numpy as np
from jax import lax

D = 2048
FF = 7168
TOP = 2
NACT = 128
STEPS = 128
EXPERTS = 4
TOK_GRP = 128
CAP = 128
TOKENS = 2048


def draw_trace_codes(key, part):
    count = TOKENS // STEPS
    key_class = jax.random.fold_in(key, 11)
    key_plain = jax.random.fold_in(key, 12)
    key_where = jax.random.fold_in(key, 13)
    key_depth = jax.random.fold_in(key, 14)
    forgetful = jax.random.randint(key_class, (count, 1), 0, 4) == 0
    plain_codes = jax.random.randint(key_plain, (count, STEPS), 1, 1025)
    lowered = jax.random.randint(key_where, (count, STEPS), 0, 64) == 0
    depth_codes = jax.random.randint(key_depth, (count, STEPS), 768, 1025)
    kept_codes = jnp.where(lowered, depth_codes, 1024)
    codes = jnp.where(forgetful, plain_codes, kept_codes)
    return codes.reshape(-1).astype(jnp.int32)


def set_ends(values, rng, least, top_value):
    spot = [jax.random.randint(jax.random.fold_in(rng, axis), (), 0, length) for axis, length in enumerate(values.shape)]
    longest = values.shape.index(max(values.shape))
    beside = spot[:longest] + [(spot[longest] + 1) % values.shape[longest]] + spot[longest + 1:]
    return values.at[tuple(spot)].set(least).at[tuple(beside)].set(top_value)


def block_levels(key, extent, cuts, least, largest):
    level, own = 1.0, jax.random.fold_in(key, 6)
    for dim, shards_of in cuts:
        heights = jnp.exp(jax.random.uniform(jax.random.fold_in(own, dim), (shards_of,), jnp.float32, least / len(cuts), largest / len(cuts)))
        level = level * jnp.repeat(heights, extent[dim] // shards_of).reshape([-1 if axis == dim else 1 for axis in range(len(extent))])
    return level


def deal_out(stream_key, own, number, rows, count, top, most, skew):
    ranking = jax.random.permutation(stream_key, count)
    heavy_load, usual = portions_of(count, rows * top, most, skew, True), portions_of(count, rows * top, most, skew, False)
    places = jnp.arange(count)

    def named(lengths, turn):
        used = int((lengths > 0).sum())
        fixed = max(1, used // 4)
        passed = fixed + (places - fixed + turn * (used - fixed)) % max(1, count - fixed)
        return jnp.zeros((count,), jnp.int32).at[ranking[jnp.where(places < fixed, places, passed)]].set(jnp.asarray(lengths, jnp.int32))

    lengths = jnp.where(number % 4 == 0, named(heavy_load, number // 4), named(usual, number - number // 4 - 1))
    mixed = jax.random.permutation(jax.random.fold_in(own, 3), count)
    giver, receiver = mixed[0:count // 2 * 2:2], mixed[1:count // 2 * 2:2]
    room = jnp.minimum(lengths[giver] - 1, most - lengths[receiver]) // 2
    room = jnp.where((giver == ranking[0]) | (receiver == ranking[0]) | (lengths[receiver] == 0), 0, jnp.maximum(room, 0))
    passed = jax.random.randint(jax.random.fold_in(own, 4), (count // 2,), 0, 1 << 20) % (room + 1)
    lengths = lengths.at[giver].add(-passed).at[receiver].add(passed)
    items = jnp.searchsorted(jnp.cumsum(lengths), jnp.arange(rows * top), side="right").astype(jnp.int32)
    table = items.reshape(top, rows).T
    table = table[jax.random.permutation(jax.random.fold_in(own, 1), rows)]
    turn = jax.random.randint(jax.random.fold_in(own, 2), (rows, 1), 0, top)
    return jnp.take_along_axis(table, (jnp.arange(top)[None, :] + turn) % top, axis=1)


def portions_of(number_of, total, most, slope, full):
    loads = [(1 << 20) // math.isqrt(standing ** slope) + 1 for standing in range(1, number_of + 1)]
    largest = most if full else min(most, max(-(-total // number_of), total * loads[0] // sum(loads)))
    least = 1 if total - largest >= number_of - 1 else 0
    given, surplus = [largest] + [least] * (number_of - 1), total - largest - least * (number_of - 1)
    while surplus > 0:
        candidates = [i for i in range(1, number_of) if given[i] < largest] or [i for i in range(1, number_of) if given[i] < most]
        whole, remaining = sum([loads[i] for i in candidates]), surplus
        for i in candidates:
            addition = min(most - given[i], max(1, remaining * loads[i] // whole), surplus)
            given[i] = given[i] + addition
            surplus = surplus - addition
    return np.array(given)


def scatter_about(rng, extent, width, bound, shards=(), kind=jnp.bfloat16):
    values = jax.random.normal(rng, extent, jnp.float32) * width
    if len(shards) > 0:
        values = block_levels(rng, extent, shards, -0.22, 0.18) * values
    return jnp.clip(values, min=-bound, max=bound).astype(kind)


def setup_inputs(seed: int = 0) -> dict:
    key_list = jax.random.split(jax.random.key(seed), 12)
    tokens = scatter_about(key_list[0], (TOKENS, D), 1.0, 6.0, ((0, 16), (1, 2)))
    norm_gain = jnp.clip(1.0 + 0.15 * jax.random.normal(key_list[1], (D,), jnp.float32), 0.25, 1.75).astype(jnp.bfloat16)
    expert_ids_keys = jax.random.split(jax.random.fold_in(key_list[2], 1), TOKENS // TOK_GRP)
    expert_ids_turns = jax.random.permutation(jax.random.fold_in(key_list[2], 3), TOKENS // TOK_GRP)
    expert_ids = jax.vmap(lambda own, number: deal_out(jax.random.fold_in(key_list[2], 2), own, number, TOK_GRP, EXPERTS, TOP, CAP, 2))(expert_ids_keys, expert_ids_turns).reshape((TOKENS, TOP))
    gate_codes = set_ends(jax.random.randint(key_list[3], (TOKENS, TOP), 1, 256), jax.random.fold_in(key_list[3], 1), 1, 255).astype(jnp.int32)
    gate_weights = scatter_about(key_list[4], (EXPERTS, FF, D), D ** -0.5, 0.125, ((0, 4), (1, 8)))
    up_weights = scatter_about(key_list[5], (EXPERTS, FF, D), D ** -0.5, 0.125, ((0, 4), (1, 8)))
    down_weights = scatter_about(key_list[6], (EXPERTS, FF, D), FF ** -0.5, 0.0625, ((0, 4), (1, 8)))
    value_head = scatter_about(key_list[7], (D, NACT), D ** -0.5, 0.125)
    actions = set_ends(jax.random.randint(key_list[8], (TOKENS,), 0, NACT), jax.random.fold_in(key_list[8], 1), 0, NACT - 1).astype(jnp.int32)
    rewards = set_ends(jax.random.randint(key_list[9], (TOKENS,), -8, 9), jax.random.fold_in(key_list[9], 1), -8, 8).astype(jnp.int32)
    trace_codes = draw_trace_codes(jax.random.fold_in(key_list[11], 71), 0)
    return dict(tokens=tokens, norm_gain=norm_gain, expert_ids=expert_ids, gate_codes=gate_codes, gate_weights=gate_weights, up_weights=up_weights, down_weights=down_weights, value_head=value_head, actions=actions, rewards=rewards, trace_codes=trace_codes)


DISCOUNT = 0.99
EPSILON = 1e-05

def expert_rows(row_block, gate_matrix, lift_matrix, down_matrix):
    gate_value = lax.dot_general(row_block, gate_matrix, (((1,), (1,)), ((), ())), preferred_element_type=jnp.float32)
    lift_value = lax.dot_general(row_block, lift_matrix, (((1,), (1,)), ((), ())), preferred_element_type=jnp.float32)
    hidden = (jax.nn.silu(gate_value) * lift_value).astype(jnp.bfloat16)
    return jnp.dot(hidden, down_matrix, preferred_element_type=jnp.float32)

def retrace(action_values, actions, rewards, trace_codes):
    greedy = lax.optimization_barrier(jnp.max(action_values, axis=1))
    picked = (actions[:, None] == jnp.arange(action_values.shape[1], dtype=jnp.int32)[None, :]).astype(jnp.float32)
    taken = lax.optimization_barrier(jnp.sum(action_values * picked, axis=1))
    trace = trace_codes.astype(jnp.float32) / 1024.0
    reward = rewards.astype(jnp.float32) * 0.25
    greedy = greedy.reshape(-1, STEPS)
    taken = taken.reshape(-1, STEPS)
    trace = trace.reshape(-1, STEPS)
    reward = reward.reshape(-1, STEPS)
    padding = jnp.zeros_like(greedy[:, :1])
    greedy_next = jnp.concatenate([greedy[:, 1:], padding], axis=1)
    taken_next = jnp.concatenate([taken[:, 1:], padding], axis=1)
    trace_next = jnp.concatenate([trace[:, 1:], padding], axis=1)
    driver = reward + DISCOUNT * (greedy_next - trace_next * taken_next)
    log_sums = jnp.cumsum(jnp.log(DISCOUNT * trace), axis=1)
    spans = log_sums[:, None, :] - log_sums[:, :, None]
    upper_mask = jnp.arange(STEPS, dtype=jnp.int32)[None, :] >= jnp.arange(STEPS, dtype=jnp.int32)[:, None]
    weight = jnp.where(upper_mask[None, :, :], jnp.exp(jnp.minimum(spans, 0.0)), 0.0)
    target = jnp.einsum('nts,ns->nt', weight, driver, precision=lax.Precision.HIGHEST)
    return target.reshape(-1)

def reference(tokens, norm_gain, expert_ids, gate_codes, gate_weights, up_weights, down_weights, value_head, actions, rewards, trace_codes):
    widened = tokens.astype(jnp.float32)
    scaling = lax.rsqrt(lax.optimization_barrier(jnp.mean(widened * widened, axis=1, keepdims=True)) + EPSILON)
    normed = (widened * scaling * norm_gain.astype(jnp.float32)[None, :]).astype(jnp.bfloat16)
    codes = gate_codes.astype(jnp.float32)
    gate_share = codes / lax.optimization_barrier(jnp.sum(codes, axis=1, keepdims=True))
    row_limit = TOKENS // TOK_GRP * CAP

    def one_expert(running, inputs):
        expert_index, gate_matrix, lift_matrix, down_matrix = inputs
        matched = expert_ids == expert_index
        share = lax.optimization_barrier(jnp.sum(jnp.where(matched, gate_share, 0.0), axis=1))
        chosen = jnp.any(matched, axis=1)
        chosen_rows = jnp.nonzero(chosen, size=row_limit, fill_value=0)[0].astype(jnp.int32)
        amount = jnp.sum(chosen.astype(jnp.int32))
        in_range = (jnp.arange(row_limit, dtype=jnp.int32) < amount).astype(jnp.float32)
        output = expert_rows(normed[chosen_rows], gate_matrix, lift_matrix, down_matrix)
        running = running.at[chosen_rows].add(output * (share[chosen_rows] * in_range)[:, None])
        return (running, None)
    start_sum = jnp.zeros((TOKENS, D), jnp.float32)
    blended, _ = lax.scan(one_expert, start_sum, (jnp.arange(EXPERTS, dtype=jnp.int32), gate_weights, up_weights, down_weights))
    action_values = jnp.dot(blended, value_head.astype(jnp.float32), precision=lax.Precision.HIGHEST, preferred_element_type=jnp.float32)
    retrace_targets = retrace(action_values, actions, rewards, trace_codes)
    return (action_values, retrace_targets)
```

```python
import jax
import jax.numpy as jnp
from jax import lax
from jax.sharding import PartitionSpec as P

STEPS = 128
DISCOUNT = 0.99
EPSILON = 1e-05


def send(block, axis, step, back=False):
    count = lax.axis_size(axis)
    if count & (count - 1) == 0:
        pairs = [(i, i ^ step) for i in range(count)]
    else:
        turn = -step if back else step
        pairs = [(i, (i + turn) % count) for i in range(count)]
    return lax.ppermute(block, axis, pairs)


def origin(axis, step):
    count = lax.axis_size(axis)
    here = lax.axis_index(axis)
    if count & (count - 1) == 0:
        return here ^ step
    return (here - step) % count


def spread(block):
    count = lax.axis_size("dp")
    if count != 4:
        return [block] + [send(block, "dp", step) for step in range(1, count)]
    beside = send(block, "dp", 1)
    above = send(block, "dp", 2)
    half = block.shape[0] // 2
    corner = jnp.concatenate(
        [send(beside[:half], "dp", 2), send(above[half:], "dp", 1)], axis=0
    )
    return [block, beside, above, corner]


def retrace(action_values, actions, rewards, trace_codes):
    greedy = jnp.max(action_values, axis=1)
    picked = (
        actions[:, None] == jnp.arange(action_values.shape[1], dtype=jnp.int32)[None, :]
    ).astype(jnp.float32)
    taken = jnp.sum(action_values * picked, axis=1)
    trace = trace_codes.astype(jnp.float32) / 1024.0
    reward = rewards.astype(jnp.float32) * 0.25
    greedy = greedy.reshape(-1, STEPS)
    taken = taken.reshape(-1, STEPS)
    trace = trace.reshape(-1, STEPS)
    reward = reward.reshape(-1, STEPS)
    padding = jnp.zeros_like(greedy[:, :1])
    greedy_next = jnp.concatenate([greedy[:, 1:], padding], axis=1)
    taken_next = jnp.concatenate([taken[:, 1:], padding], axis=1)
    trace_next = jnp.concatenate([trace[:, 1:], padding], axis=1)
    driver = reward + DISCOUNT * (greedy_next - trace_next * taken_next)
    log_sums = jnp.cumsum(jnp.log(DISCOUNT * trace), axis=1)
    spans = log_sums[:, None, :] - log_sums[:, :, None]
    upper_mask = (
        jnp.arange(STEPS, dtype=jnp.int32)[None, :] >= jnp.arange(STEPS, dtype=jnp.int32)[:, None]
    )
    weight = jnp.where(upper_mask[None, :, :], jnp.exp(jnp.minimum(spans, 0.0)), 0.0)
    target = jnp.einsum("nts,ns->nt", weight, driver, precision=lax.Precision.HIGHEST)
    return target.reshape(-1)


def dot_rows(rows, matrix):
    return lax.dot_general(
        rows, matrix, (((1,), (1,)), ((), ())), preferred_element_type=jnp.float32
    )


def per_device(
    tokens,
    norm_gain,
    expert_ids,
    gate_codes,
    gate_weights,
    up_weights,
    down_weights,
    value_head,
    actions,
    rewards,
    trace_codes,
):
    groups = lax.axis_size("expert")
    dps = lax.axis_size("dp")
    rows, width = tokens.shape
    acts = value_head.shape[1]
    halves = lax.axis_size("tensor")
    core = lax.axis_index("tensor")
    part = rows // halves
    gate_w, up_w = gate_weights[0], up_weights[0]
    gain = norm_gain.astype(jnp.float32)[None, :]

    folded = jnp.dot(down_weights[0], value_head, preferred_element_type=jnp.float32)
    folded_hi = folded.astype(jnp.bfloat16)
    folded_lo = (folded - folded_hi.astype(jnp.float32)).astype(jnp.bfloat16)
    folded_pair = jnp.concatenate([folded_hi, folded_lo], axis=1)

    def compute(near, far):
        first = jnp.where(core == 0, near, far)
        second = jnp.where(core == 0, far, near)
        wide = jnp.concatenate([first, second], axis=1).astype(jnp.float32)
        scaling = lax.rsqrt(jnp.mean(wide * wide, axis=1, keepdims=True) + EPSILON)
        normed = (wide * scaling * gain).astype(jnp.bfloat16)
        hidden = (jax.nn.silu(dot_rows(normed, gate_w)) * dot_rows(normed, up_w)).astype(
            jnp.bfloat16
        )
        both = jnp.dot(hidden, folded_pair, preferred_element_type=jnp.float32)
        return both[:, :acts] + both[:, acts:]

    codes = gate_codes.astype(jnp.float32)
    gate_share = codes / jnp.sum(codes, axis=1, keepdims=True)

    stages = []
    for step in range(groups):
        block = tokens if step == 0 else send(tokens, "expert", step)
        stages.append(spread(block))
    blended = None
    for step in range(groups):
        near = jnp.concatenate(stages[step], axis=0)
        far = send(near, "tensor", 1)
        partial = compute(near, far).reshape(dps, halves, part, acts)
        keep = jnp.where(core == 0, partial[:, 0], partial[:, 1])
        give = jnp.where(core == 0, partial[:, 1], partial[:, 0])
        keep = keep + send(give, "tensor", 1)
        total = keep[0]
        for other in range(1, dps):
            total = total + send(keep[other], "dp", other, back=True)
        if step:
            total = send(total, "expert", step, back=True)
        if groups & (groups - 1) == 0:
            expert = lax.axis_index("expert") ^ step
        else:
            expert = (lax.axis_index("expert") + step) % groups
        share = jnp.sum(jnp.where(expert_ids == expert, gate_share, 0.0), axis=1)
        share = jnp.where(core == 0, share[:part], share[part:])
        piece = total * share[:, None]
        blended = piece if blended is None else blended + piece
    other_half = send(blended, "tensor", 1)
    action_values = jnp.concatenate(
        [jnp.where(core == 0, blended, other_half), jnp.where(core == 0, other_half, blended)],
        axis=0,
    )
    retrace_targets = retrace(action_values, actions, rewards, trace_codes)
    return (action_values, retrace_targets)


def solution(mesh):
    in_specs = (
        P(("dp", "expert"), "tensor"),
        P(),
        P(("dp", "expert"), None),
        P(("dp", "expert"), None),
        P("expert", ("dp", "tensor"), None),
        P("expert", ("dp", "tensor"), None),
        P("expert", ("dp", "tensor"), None),
        P(),
        P(("dp", "expert")),
        P(("dp", "expert")),
        P(("dp", "expert")),
    )
    out_specs = (P(("dp", "expert"), None), P(("dp", "expert")))
    return jax.shard_map(
        per_device, mesh=mesh, in_specs=in_specs, out_specs=out_specs, check_vma=False
    )
```

```python
import jax
import jax.numpy as jnp
from jax import lax
from jax.experimental import pallas as pl
from jax.experimental.pallas import tpu as pltpu
from jax.sharding import PartitionSpec as P

STEPS = 128
DISCOUNT = 0.99
EPSILON = 1e-05


def send(block, axis, step, back=False):
    count = lax.axis_size(axis)
    if count & (count - 1) == 0:
        pairs = [(i, i ^ step) for i in range(count)]
    else:
        turn = -step if back else step
        pairs = [(i, (i + turn) % count) for i in range(count)]
    return lax.ppermute(block, axis, pairs)


def spread(block, held=None):
    count = lax.axis_size("dp")
    if count != 4:
        return [block] + [send(block, "dp", step) for step in range(1, count)]
    beside = send(block, "dp", 1)
    above = send(block, "dp", 2)
    half = block.shape[0] // 2
    if held is not None:
        beside, above, _ = lax.optimization_barrier((beside, above, held))
    corner = jnp.concatenate(
        [send(beside[:half], "dp", 2), send(above[half:], "dp", 1)], axis=0
    )
    return [block, beside, above, corner]


def retrace(action_values, actions, rewards, trace_codes):
    greedy = jnp.max(action_values, axis=1)
    picked = (
        actions[:, None] == jnp.arange(action_values.shape[1], dtype=jnp.int32)[None, :]
    ).astype(jnp.float32)
    taken = jnp.sum(action_values * picked, axis=1)
    trace = trace_codes.astype(jnp.float32) / 1024.0
    reward = rewards.astype(jnp.float32) * 0.25
    greedy = greedy.reshape(-1, STEPS)
    taken = taken.reshape(-1, STEPS)
    trace = trace.reshape(-1, STEPS)
    reward = reward.reshape(-1, STEPS)
    padding = jnp.zeros_like(greedy[:, :1])
    greedy_next = jnp.concatenate([greedy[:, 1:], padding], axis=1)
    taken_next = jnp.concatenate([taken[:, 1:], padding], axis=1)
    trace_next = jnp.concatenate([trace[:, 1:], padding], axis=1)
    driver = reward + DISCOUNT * (greedy_next - trace_next * taken_next)
    log_sums = jnp.cumsum(jnp.log(DISCOUNT * trace), axis=1)
    spans = log_sums[:, None, :] - log_sums[:, :, None]
    upper_mask = (
        jnp.arange(STEPS, dtype=jnp.int32)[None, :] >= jnp.arange(STEPS, dtype=jnp.int32)[:, None]
    )
    weight = jnp.where(upper_mask[None, :, :], jnp.exp(jnp.minimum(spans, 0.0)), 0.0)
    target = jnp.einsum("nts,ns->nt", weight, driver, precision=lax.Precision.HIGHEST)
    return target.reshape(-1)


def dot_rows(rows, matrix):
    return lax.dot_general(
        rows, matrix, (((1,), (1,)), ((), ())), preferred_element_type=jnp.float32
    )


def expert_kernel(
    core_ref, near_ref, far_ref, gain_near, gain_far, gate_near, gate_far, up_near, up_far,
    folded_ref, out_ref, near_rows, far_rows, total,
):
    step = pl.program_id(1)
    acts = out_ref.shape[1]
    tile = gate_near.shape[0]

    @pl.when(step == 0)
    def _():
        near = near_ref[...].astype(jnp.float32)
        far = far_ref[...].astype(jnp.float32)
        squares = jnp.sum(near * near + far * far, axis=1, keepdims=True)
        scaling = lax.rsqrt(squares / (2 * near.shape[1]) + EPSILON)
        near_rows[...] = (near * scaling * gain_near[...].astype(jnp.float32)).astype(jnp.bfloat16)
        far_rows[...] = (far * scaling * gain_far[...].astype(jnp.float32)).astype(jnp.bfloat16)

    near_w = jnp.concatenate([gate_near[...], up_near[...]], axis=0)
    far_w = jnp.concatenate([gate_far[...], up_far[...]], axis=0)
    both = dot_rows(near_rows[...], near_w) + dot_rows(far_rows[...], far_w)
    gate, up = both[:, :tile], both[:, tile:]
    hidden = (gate / (1.0 + jnp.exp(-gate)) * up).astype(jnp.bfloat16)
    piece = jnp.dot(hidden, folded_ref[...], preferred_element_type=jnp.float32)

    @pl.when(step == 0)
    def _():
        total[...] = piece

    @pl.when(step > 0)
    def _():
        total[...] += piece

    @pl.when(step == pl.num_programs(1) - 1)
    def _():
        out_ref[...] = total[:, :acts] + total[:, acts:]


def expert_values(core, near, far, gain, gate_w, up_w, folded_pair):
    rows, width = near.shape
    hidden = gate_w.shape[0]
    acts = folded_pair.shape[1] // 2
    tile = 128 if hidden % 128 == 0 else hidden
    height = 1024 if rows % 1024 == 0 else rows
    whole = pl.BlockSpec((height, width), lambda i, j, c: (i, 0))
    gain_n = pl.BlockSpec((1, width), lambda i, j, c: (0, c[0]))
    gain_f = pl.BlockSpec((1, width), lambda i, j, c: (0, 1 - c[0]))
    w_n = pl.BlockSpec((tile, width), lambda i, j, c: (j, c[0]))
    w_f = pl.BlockSpec((tile, width), lambda i, j, c: (j, 1 - c[0]))
    return pl.pallas_call(
        expert_kernel,
        grid_spec=pltpu.PrefetchScalarGridSpec(
            num_scalar_prefetch=1,
            grid=(rows // height, hidden // tile),
            in_specs=[
                whole, whole, gain_n, gain_f, w_n, w_f, w_n, w_f,
                pl.BlockSpec((tile, 2 * acts), lambda i, j, c: (j, 0)),
            ],
            out_specs=pl.BlockSpec((height, acts), lambda i, j, c: (i, 0)),
            scratch_shapes=[
                pltpu.VMEM((height, width), jnp.bfloat16),
                pltpu.VMEM((height, width), jnp.bfloat16),
                pltpu.VMEM((height, 2 * acts), jnp.float32),
            ],
        ),
        out_shape=jax.ShapeDtypeStruct((rows, acts), jnp.float32),
        cost_estimate=pl.CostEstimate(
            flops=2 * rows * hidden * (4 * width + 2 * acts),
            bytes_accessed=4 * rows * width + 8 * hidden * width,
            transcendentals=rows * hidden,
        ),
    )(core, near, far, gain, gain, gate_w, gate_w, up_w, up_w, folded_pair)


def per_device(
    tokens,
    norm_gain,
    expert_ids,
    gate_codes,
    gate_weights,
    up_weights,
    down_weights,
    value_head,
    actions,
    rewards,
    trace_codes,
):
    groups = lax.axis_size("expert")
    dps = lax.axis_size("dp")
    rows, width = tokens.shape
    acts = value_head.shape[1]
    core = lax.axis_index("tensor")
    gate_w, up_w = gate_weights[0], up_weights[0]
    gain = norm_gain[None, :]
    core_index = core.reshape(1).astype(jnp.int32)

    folded = jnp.dot(down_weights[0], value_head, preferred_element_type=jnp.float32)
    folded_hi = folded.astype(jnp.bfloat16)
    folded_lo = (folded - folded_hi.astype(jnp.float32)).astype(jnp.bfloat16)
    folded_pair = jnp.concatenate([folded_hi, folded_lo], axis=1)

    codes = gate_codes.astype(jnp.float32)
    gate_share = codes / jnp.sum(codes, axis=1, keepdims=True)

    def values(near):
        far = send(near, "tensor", 1)
        return expert_values(core_index, near, far, gain, gate_w, up_w, folded_pair)

    cut = (groups + 1) // 2
    parts = []
    blocks = [tokens if step == 0 else send(tokens, "expert", step) for step in range(groups)]
    held = None
    for span in (blocks[:cut], blocks[cut:]):
        if not span:
            continue
        stages = [spread(block, held) for block in span]
        near = jnp.concatenate([stage[other] for other in range(dps) for stage in stages], axis=0)
        found = values(near)
        held = None
        found = found.reshape(dps, len(span), rows, acts)
        total = found[0]
        for other in range(1, dps):
            total = total + send(found[other], "dp", other, back=True)
        parts.extend(total[index] for index in range(len(span)))
    total = parts
    blended = None
    for step in range(groups):
        result = send(total[step], "expert", step, back=True) if step else total[0]
        if groups & (groups - 1) == 0:
            expert = lax.axis_index("expert") ^ step
        else:
            expert = (lax.axis_index("expert") + step) % groups
        share = jnp.sum(jnp.where(expert_ids == expert, gate_share, 0.0), axis=1, keepdims=True)
        blended = result * share if blended is None else blended + result * share
    action_values = blended + send(blended, "tensor", 1)
    retrace_targets = retrace(action_values, actions, rewards, trace_codes)
    return (action_values, retrace_targets)


def solution(mesh):
    in_specs = (
        P(("dp", "expert"), "tensor"),
        P(),
        P(("dp", "expert"), None),
        P(("dp", "expert"), None),
        P("expert", ("dp", "tensor"), None),
        P("expert", ("dp", "tensor"), None),
        P("expert", ("dp", "tensor"), None),
        P(),
        P(("dp", "expert")),
        P(("dp", "expert")),
        P(("dp", "expert")),
    )
    out_specs = (P(("dp", "expert"), None), P(("dp", "expert")))
    return jax.shard_map(
        per_device, mesh=mesh, in_specs=in_specs, out_specs=out_specs, check_vma=False
    )
```
